32 devices in a mesh: dp: 8 (over y, x, core), tensor: 4 (over z).
Axes of the slice: x: 2, y: 2, z: 4, core: 2. Of those that a mesh axis runs over, the one named last changes fastest.
Arguments:
- layer_input: float32 [2048, 768], P(('dp', 'tensor')), may hold values from -6 to 6
- segments: int32 [8, 256], P('dp'), may hold values from 0 to 2, as said below
- routes: int32 [2048, 2], P('dp'), may hold values from 0 to 15, all different within a row; in each aligned block of 256 rows (0 to 255, 256 to 511, ...) at most 48 rows name the same one
- gate_weights: float32 [2048, 2], P('dp'), may hold values from 0.2 to 1
- first_gain: bfloat16 [768], P(('dp', 'tensor')), may hold values from 0.5 to 1.5
- first_query: bfloat16 [768, 768], P('dp', 'tensor'), may hold values from -0.21875 to 0.21875
- first_key: bfloat16 [768, 768], P('dp', 'tensor'), may hold values from -0.21875 to 0.21875
- first_value: bfloat16 [768, 768], P('dp', 'tensor'), may hold values from -0.21875 to 0.21875
- first_output: bfloat16 [768, 768], P('tensor', 'dp'), may hold values from -0.875 to 0.875
- first_bias: bfloat16 [32, 12], P('dp', 'tensor'), may hold values from -2 to 300
- first_dense_gain: bfloat16 [768], P(('dp', 'tensor')), may hold values from 0.5 to 1.5
- first_dense_up: bfloat16 [768, 3072], P('dp', 'tensor'), may hold values from -0.21875 to 0.21875
- first_dense_down: bfloat16 [3072, 768], P('tensor', 'dp'), may hold values from -0.109375 to 0.109375
- second_gain: bfloat16 [768], P(('dp', 'tensor')), may hold values from 0.5 to 1.5
- second_query: bfloat16 [768, 768], P('dp', 'tensor'), may hold values from -0.21875 to 0.21875
- second_key: bfloat16 [768, 768], P('dp', 'tensor'), may hold values from -0.21875 to 0.21875
- second_value: bfloat16 [768, 768], P('dp', 'tensor'), may hold values from -0.21875 to 0.21875
- second_output: bfloat16 [768, 768], P('tensor', 'dp'), may hold values from -0.875 to 0.875
- second_bias: bfloat16 [32, 12], P('dp', 'tensor'), may hold values from -2 to 300
- second_expert_gain: bfloat16 [768], P(('dp', 'tensor')), may hold values from 0.5 to 1.5
- expert_up: bfloat16 [16, 768, 3072], P('dp', None, 'tensor'), may hold values from -0.21875 to 0.21875
- expert_down: bfloat16 [16, 3072, 768], P('dp', 'tensor'), may hold values from -0.109375 to 0.109375
- output_grad: float32 [2048, 768], P(('dp', 'tensor')), may hold values from -6 to 6
Outputs:
- layer_output: float32 [2048, 768], P(('dp', 'tensor'))
- input_grad: float32 [2048, 768], P(('dp', 'tensor'))
- first_gain_grad: float32 [768], P(('dp', 'tensor'))
- first_query_grad: float32 [768, 768], P('dp', 'tensor')
- first_key_grad: float32 [768, 768], P('dp', 'tensor')
- first_value_grad: float32 [768, 768], P('dp', 'tensor')
- first_output_grad: float32 [768, 768], P('tensor', 'dp')
- first_bias_grad: float32 [32, 12], P('dp', 'tensor')
- first_dense_gain_grad: float32 [768], P(('dp', 'tensor'))
- first_dense_up_grad: float32 [768, 3072], P('dp', 'tensor')
- first_dense_down_grad: float32 [3072, 768], P('tensor', 'dp')
- second_gain_grad: float32 [768], P(('dp', 'tensor'))
- second_query_grad: float32 [768, 768], P('dp', 'tensor')
- second_key_grad: float32 [768, 768], P('dp', 'tensor')
- second_value_grad: float32 [768, 768], P('dp', 'tensor')
- second_output_grad: float32 [768, 768], P('tensor', 'dp')
- second_bias_grad: float32 [32, 12], P('dp', 'tensor')
- second_expert_gain_grad: float32 [768], P(('dp', 'tensor'))
- expert_up_grad: float32 [16, 768, 3072], P('dp', None, 'tensor')
- expert_down_grad: float32 [16, 3072, 768], P('dp', 'tensor')
The draws below stay inside these ranges and needn't reach their ends.
Inputs may be any that keep to these rules, and one draw needn't show every extreme that they name: `segments`: documents of at most 2000 tokens, and at least 200 except where cut, are laid end to end over all sequences in order, so a sequence's first and last documents may be cut short. Within a sequence segment numbers start at 0 and never fall. `routes`: each token names 2 different experts. Within one sequence's 256 tokens no expert is named more than 48 times, a bound that some block reaches.
All inputs are finite; a program needn't handle non-finite values.
Results may differ from the reference program's by a relative error of at most 0.024.
Values may be sent and summed in bfloat16 or wider, within the bound.
A program may use at most 128 MiB of HBM per device.

```python
import math
import jax
import jax.numpy as jnp
import numpy as np
from jax import lax

D = 768
H = 12
DH = 64
FF = 3072
TOP = 2
BUCKETS = 32
DOC_MIN = 200
DOC_MAX = 2000
SEQ = 256
EXPERTS = 16
SEQS = 8
TOKENS = 2048
CAP = 48


def spiked_table(key):
    base_key = jax.random.fold_in(key, 1)
    bias_table = jax.random.uniform(base_key, (BUCKETS, H), jnp.float32, -2.0, 2.0)
    return bias_table


def draw_first_bias(key, part):
    return spiked_table(jax.random.fold_in(key, 11)).astype(jnp.bfloat16)


def draw_second_bias(key, part):
    return spiked_table(jax.random.fold_in(key, 12)).astype(jnp.bfloat16)


def draw_segments(key, part):
    doc_count = TOKENS // DOC_MIN + 2
    short_docs = (SEQ - 2) // DOC_MIN
    doc_lengths = jax.random.randint(jax.random.fold_in(key, 21), (doc_count,), DOC_MIN, DOC_MAX + 1, jnp.int32)
    doc_numbers = jnp.arange(doc_count, dtype=jnp.int32)
    exact_docs = (doc_numbers >= 1) & (doc_numbers <= short_docs)
    doc_lengths = jnp.where(exact_docs, jnp.int32(DOC_MIN), doc_lengths)
    start_shift = doc_lengths[0] - 1
    doc_ends = jnp.cumsum(doc_lengths) - start_shift
    positions = jnp.arange(TOKENS, dtype=jnp.int32)
    doc_of = jnp.sum((doc_ends[None, :] <= positions[:, None]).astype(jnp.int32), axis=1)
    per_sequence = doc_of.reshape(SEQS, SEQ)
    return per_sequence - per_sequence[:, :1]


def shard_levels(stream_key, extent, split, least, top_value):
    loudness, own = 1.0, jax.random.fold_in(stream_key, 6)
    for position, parts in split:
        steps = jnp.exp(jax.random.uniform(jax.random.fold_in(own, position), (parts,), jnp.float32, least / len(split), top_value / len(split)))
        loudness = loudness * jnp.repeat(steps, extent[position] // parts).reshape([-1 if axis == position else 1 for axis in range(len(extent))])
    return loudness


def routed_block(rng, own, number, rows, count, top, limit, slope):
    order = jax.random.permutation(rng, count)
    crowded, usual = load_shares(count, rows * top, limit, slope, True), load_shares(count, rows * top, limit, slope, False)
    places = jnp.arange(count)

    def named(sizes, offset_by):
        used = int((sizes > 0).sum())
        fixed = max(1, used // 4)
        moved = fixed + (places - fixed + offset_by * (used - fixed)) % max(1, count - fixed)
        return jnp.zeros((count,), jnp.int32).at[order[jnp.where(places < fixed, places, moved)]].set(jnp.asarray(sizes, jnp.int32))

    sizes = jnp.where(number % 4 == 0, named(crowded, number // 4), named(usual, number - number // 4 - 1))
    mixed = jax.random.permutation(jax.random.fold_in(own, 3), count)
    source_of, sink = mixed[0:count // 2 * 2:2], mixed[1:count // 2 * 2:2]
    margin = jnp.minimum(sizes[source_of] - 1, limit - sizes[sink]) // 2
    margin = jnp.where((source_of == order[0]) | (sink == order[0]) | (sizes[sink] == 0), 0, jnp.maximum(margin, 0))
    moved = jax.random.randint(jax.random.fold_in(own, 4), (count // 2,), 0, 1 << 20) % (margin + 1)
    sizes = sizes.at[source_of].add(-moved).at[sink].add(moved)
    members = jnp.searchsorted(jnp.cumsum(sizes), jnp.arange(rows * top), side="right").astype(jnp.int32)
    table = members.reshape(top, rows).T
    table = table[jax.random.permutation(jax.random.fold_in(own, 1), rows)]
    offset_by = jax.random.randint(jax.random.fold_in(own, 2), (rows, 1), 0, top)
    return jnp.take_along_axis(table, (jnp.arange(top)[None, :] + offset_by) % top, axis=1)


def load_shares(number_of, total, limit, skew, full):
    weights = [(1 << 20) // math.isqrt(standing ** skew) + 1 for standing in range(1, number_of + 1)]
    largest = limit if full else min(limit, max(-(-total // number_of), total * weights[0] // sum(weights)))
    least = 1 if total - largest >= number_of - 1 else 0
    counts, spare = [largest] + [least] * (number_of - 1), total - largest - least * (number_of - 1)
    while spare > 0:
        movable = [i for i in range(1, number_of) if counts[i] < largest] or [i for i in range(1, number_of) if counts[i] < limit]
        pool, left = sum([weights[i] for i in movable]), spare
        for i in movable:
            more = min(limit - counts[i], max(1, left * weights[i] // pool), spare)
            counts[i] = counts[i] + more
            spare = spare - more
    return np.array(counts)


def gaussian(stream_key, extent, width, bound, pieces=(), kind=jnp.bfloat16):
    factor_of = shard_levels(stream_key, extent, pieces, -0.22, 0.18) if pieces else 1.0
    values = jax.random.normal(stream_key, extent, jnp.float32) * width * factor_of
    return jnp.minimum(jnp.maximum(values, -bound), bound).astype(kind)


def setup_inputs(seed: int = 0) -> dict:
    splits = jax.random.split(jax.random.key(seed), 24)
    layer_input = gaussian(splits[0], (TOKENS, D), 1.0, 6.0, ((0, 32),), jnp.float32)
    segments = draw_segments(jax.random.fold_in(splits[23], 71), 0)
    routes_keys = jax.random.split(jax.random.fold_in(splits[2], 1), TOKENS // SEQ)
    routes_turns = jax.random.permutation(jax.random.fold_in(splits[2], 3), TOKENS // SEQ)
    routes = jax.vmap(lambda own, number: routed_block(jax.random.fold_in(splits[2], 2), own, number, SEQ, EXPERTS, TOP, CAP, 2))(routes_keys, routes_turns).reshape((TOKENS, TOP))
    gate_weights = jnp.clip(0.2 + 0.8 * jax.random.uniform(splits[3], (TOKENS, TOP), jnp.float32) ** shard_levels(splits[3], (TOKENS, TOP), ((0, 8),), -0.2, 0.2), 0.2, 1.0)
    first_gain = jnp.clip(1.0 + 0.1 * jax.random.normal(splits[4], (D,), jnp.float32), 0.5, 1.5).astype(jnp.bfloat16)
    first_query = gaussian(splits[5], (D, H * DH), D ** -0.5, 0.21875, ((0, 8), (1, 4)))
    first_key = gaussian(splits[6], (D, H * DH), D ** -0.5, 0.21875, ((0, 8), (1, 4)))
    first_value = gaussian(splits[7], (D, H * DH), D ** -0.5, 0.21875, ((0, 8), (1, 4)))
    first_output = gaussian(splits[8], (H * DH, D), (H * DH * 16 // SEQ) ** -0.5, 0.875, ((0, 4), (1, 8)))
    first_bias = draw_first_bias(jax.random.fold_in(splits[23], 71), 0)
    first_dense_gain = jnp.clip(1.0 + 0.1 * jax.random.normal(splits[10], (D,), jnp.float32), 0.5, 1.5).astype(jnp.bfloat16)
    first_dense_up = gaussian(splits[11], (D, FF), D ** -0.5, 0.21875, ((0, 8), (1, 4)))
    first_dense_down = gaussian(splits[12], (FF, D), FF ** -0.5, 0.109375, ((0, 4), (1, 8)))
    second_gain = jnp.clip(1.0 + 0.1 * jax.random.normal(splits[13], (D,), jnp.float32), 0.5, 1.5).astype(jnp.bfloat16)
    second_query = gaussian(splits[14], (D, H * DH), D ** -0.5, 0.21875, ((0, 8), (1, 4)))
    second_key = gaussian(splits[15], (D, H * DH), D ** -0.5, 0.21875, ((0, 8), (1, 4)))
    second_value = gaussian(splits[16], (D, H * DH), D ** -0.5, 0.21875, ((0, 8), (1, 4)))
    second_output = gaussian(splits[17], (H * DH, D), (H * DH * 16 // SEQ) ** -0.5, 0.875, ((0, 4), (1, 8)))
    second_bias = draw_second_bias(jax.random.fold_in(splits[23], 71), 0)
    second_expert_gain = jnp.clip(1.0 + 0.1 * jax.random.normal(splits[19], (D,), jnp.float32), 0.5, 1.5).astype(jnp.bfloat16)
    expert_up = gaussian(splits[20], (EXPERTS, D, FF), D ** -0.5, 0.21875, ((0, 8), (2, 4)))
    expert_down = gaussian(splits[21], (EXPERTS, FF, D), FF ** -0.5, 0.109375, ((0, 8), (1, 4)))
    output_grad = gaussian(splits[22], (TOKENS, D), 1.0, 6.0, ((0, 32),), jnp.float32)
    return dict(layer_input=layer_input, segments=segments, routes=routes, gate_weights=gate_weights, first_gain=first_gain, first_query=first_query, first_key=first_key, first_value=first_value, first_output=first_output, first_bias=first_bias, first_dense_gain=first_dense_gain, first_dense_up=first_dense_up, first_dense_down=first_dense_down, second_gain=second_gain, second_query=second_query, second_key=second_key, second_value=second_value, second_output=second_output, second_bias=second_bias, second_expert_gain=second_expert_gain, expert_up=expert_up, expert_down=expert_down, output_grad=output_grad)


EPSILON = 1e-06
NEG_FILL = -1e+30
HALF_ROOT = 0.7071067811865476
BELL_SCALE = 0.3989422804014327

def bucket_index(length, buckets):
    exact_count = buckets // 2
    distance = np.arange(length)
    result = np.minimum(distance, exact_count)
    for bucket_level in range(1, exact_count):
        threshold = int(np.ceil(exact_count * (128.0 / exact_count) ** (bucket_level / exact_count)))
        result = result + (distance >= threshold)
    return result.astype(np.int32)

def round_trip(values):
    return lax.optimization_barrier(values.astype(jnp.bfloat16)).astype(jnp.float32)

def gelu_value(inputs):
    return 0.5 * inputs * (1.0 + lax.erf(inputs * HALF_ROOT))

def gelu_slope(inputs):
    return 0.5 * (1.0 + lax.erf(inputs * HALF_ROOT)) + inputs * jnp.exp(-0.5 * inputs * inputs) * BELL_SCALE

def product(left, right):
    return jnp.dot(left, right, preferred_element_type=jnp.float32)

def norm_forward(hidden, norm_gain):
    rounded = round_trip(hidden)
    inv_rms = lax.rsqrt(lax.optimization_barrier(jnp.mean(rounded * rounded, axis=-1, keepdims=True)) + EPSILON)
    normal = rounded * inv_rms
    return ((normal * norm_gain.astype(jnp.float32)).astype(jnp.bfloat16), normal, inv_rms)

def norm_backward(grad_normed, normal, inv_rms, norm_gain):
    grad_normal = grad_normed * norm_gain.astype(jnp.float32)
    grad_hidden = inv_rms * (grad_normal - normal * lax.optimization_barrier(jnp.mean(grad_normal * normal, axis=-1, keepdims=True)))
    return (grad_hidden, lax.optimization_barrier(jnp.sum(grad_normed * normal, axis=0)))

def relative_layout():
    buckets_of = bucket_index(SEQ, BUCKETS)
    distance = np.arange(SEQ)[:, None] - np.arange(SEQ)[None, :]
    return (buckets_of[np.maximum(distance, 0)], distance >= 0)

def bias_matrix(bias_table, index_table):
    return jnp.transpose(bias_table[index_table], (2, 0, 1))

def sequence_scores(queries, key_rows, seg_row, bias_table):
    index_table, causal = relative_layout()
    scores = jnp.einsum('ihd,jhd->hij', queries.astype(jnp.float32), key_rows.astype(jnp.float32)) / math.sqrt(DH)
    scores = scores + bias_matrix(bias_table, index_table)
    allowed = jnp.asarray(causal) & (seg_row[:, None] == seg_row[None, :])
    return jnp.where(allowed[None], scores, NEG_FILL)

def attention_layer(hidden, segments, norm_gain, query_w, key_w, value_w, output_w, bias_w):
    normed, normal, inv_rms = norm_forward(hidden, norm_gain)
    head_shape = (SEQS, SEQ, H, DH)
    query_rows = product(normed, query_w).astype(jnp.bfloat16).reshape(head_shape)
    key_rows = product(normed, key_w).astype(jnp.bfloat16).reshape(head_shape)
    value_rows = product(normed, value_w).astype(jnp.bfloat16).reshape(head_shape)
    bias_table = bias_w.astype(jnp.float32)

    def one_sequence(pack):
        queries, key_seq, value_seq, seg_row = pack
        scores = sequence_scores(queries, key_seq, seg_row, bias_table)
        highest = lax.optimization_barrier(jnp.max(scores, axis=-1, keepdims=True))
        exp_scores = jnp.exp(scores - highest)
        row_total = lax.optimization_barrier(jnp.sum(exp_scores, axis=-1, keepdims=True))
        shares = round_trip(exp_scores / row_total)
        mixed_rows = jnp.einsum('hij,jhd->ihd', shares, value_seq.astype(jnp.float32)).astype(jnp.bfloat16)
        return (mixed_rows, highest[:, :, 0] + jnp.log(row_total[:, :, 0]))
    mixed_rows, log_total = lax.map(one_sequence, (query_rows, key_rows, value_rows, segments))
    mixed_flat = mixed_rows.reshape(TOKENS, H * DH)
    output = hidden + product(mixed_flat, output_w)
    return (output, (normed, normal, inv_rms, query_rows, key_rows, value_rows, mixed_rows, mixed_flat, log_total))

def attention_back(cotangent, saved, segments, norm_gain, query_w, key_w, value_w, output_w, bias_w):
    normed, normal, inv_rms, query_rows, key_rows, value_rows, mixed_rows, mixed_flat, log_total = saved
    grad_low = cotangent.astype(jnp.bfloat16)
    output_grad_w = product(mixed_flat.T, grad_low)
    grad_mixed = product(grad_low, output_w.T).astype(jnp.bfloat16).reshape(SEQS, SEQ, H, DH)
    bias_table = bias_w.astype(jnp.float32)
    index_table, causal = relative_layout()
    inv_root = 1.0 / math.sqrt(DH)

    def one_sequence(pack):
        queries, key_seq, value_seq, seg_row, mixed_seq, log_seq, grad_seq = pack
        scores = sequence_scores(queries, key_seq, seg_row, bias_table)
        shares = jnp.exp(scores - log_seq[:, :, None])
        grad_wide = grad_seq.astype(jnp.float32)
        grad_values = jnp.einsum('hij,ihd->jhd', round_trip(shares), grad_wide).astype(jnp.bfloat16)
        share_grad = jnp.einsum('ihd,jhd->hij', grad_wide, value_seq.astype(jnp.float32))
        row_dot = jnp.einsum('ihd,ihd->hi', grad_wide, mixed_seq.astype(jnp.float32))
        score_grad = shares * (share_grad - row_dot[:, :, None])

        def bias_of(table_in):
            return bias_matrix(table_in, index_table)
        bias_grad = jax.vjp(bias_of, bias_table)[1](score_grad)[0]
        score_low = round_trip(score_grad)
        grad_queries = (jnp.einsum('hij,jhd->ihd', score_low, key_seq.astype(jnp.float32)) * inv_root).astype(jnp.bfloat16)
        grad_keys = (jnp.einsum('hij,ihd->jhd', score_low, queries.astype(jnp.float32)) * inv_root).astype(jnp.bfloat16)
        return (grad_queries, grad_keys, grad_values, bias_grad)
    grad_queries, grad_keys, grad_values, bias_grads = lax.map(one_sequence, (query_rows, key_rows, value_rows, segments, mixed_rows, log_total, grad_mixed))
    grad_queries = grad_queries.reshape(TOKENS, H * DH)
    grad_keys = grad_keys.reshape(TOKENS, H * DH)
    grad_values = grad_values.reshape(TOKENS, H * DH)
    query_grad = product(normed.T, grad_queries)
    key_grad = product(normed.T, grad_keys)
    value_grad = product(normed.T, grad_values)
    grad_normed = product(grad_queries, query_w.T) + product(grad_keys, key_w.T) + product(grad_values, value_w.T)
    grad_hidden, gain_grad = norm_backward(grad_normed, normal, inv_rms, norm_gain)
    return (cotangent + grad_hidden, (gain_grad, query_grad, key_grad, value_grad, output_grad_w, lax.optimization_barrier(jnp.sum(bias_grads, axis=0))))

def dense_layer(hidden, norm_gain, up_w, down_w):
    normed, normal, inv_rms = norm_forward(hidden, norm_gain)
    pre_act = product(normed, up_w)
    active = gelu_value(pre_act).astype(jnp.bfloat16)
    return (hidden + product(active, down_w), (normed, normal, inv_rms, pre_act, active))

def dense_back(cotangent, saved, norm_gain, up_w, down_w):
    normed, normal, inv_rms, pre_act, active = saved
    grad_low = cotangent.astype(jnp.bfloat16)
    down_grad = product(active.T, grad_low)
    grad_pre = (product(grad_low, down_w.T) * gelu_slope(pre_act)).astype(jnp.bfloat16)
    up_grad = product(normed.T, grad_pre)
    grad_normed = product(grad_pre, up_w.T)
    grad_hidden, gain_grad = norm_backward(grad_normed, normal, inv_rms, norm_gain)
    return (cotangent + grad_hidden, gain_grad, up_grad, down_grad)

def slot_plan(route_rows):
    flat_routes = route_rows.reshape(-1)
    onehot = (flat_routes[:, None] == jnp.arange(EXPERTS, dtype=jnp.int32)[None, :]).astype(jnp.int32)
    before = jnp.cumsum(onehot, axis=0) - onehot
    slot_ids = flat_routes * CAP + lax.optimization_barrier(jnp.sum(onehot * before, axis=1))
    slot_owner = jnp.full((EXPERTS * CAP,), SEQ * TOP, jnp.int32).at[slot_ids].set(jnp.arange(SEQ * TOP, dtype=jnp.int32))
    return (slot_ids.reshape(SEQ, TOP), slot_owner)

def take_rows(source_rows, index_rows):
    return source_rows[index_rows]

def to_experts(per_sequence):
    return per_sequence.reshape(SEQS, EXPERTS, CAP, D).transpose(1, 0, 2, 3).reshape(EXPERTS, SEQS * CAP, D)

def to_sequences(per_expert):
    return per_expert.reshape(EXPERTS, SEQS, CAP, D).transpose(1, 0, 2, 3).reshape(SEQS, EXPERTS * CAP, D)

def expert_layer(hidden, routes, gate_weights, norm_gain, expert_up, expert_down):
    normed, normal, inv_rms = norm_forward(hidden, norm_gain)
    slot_ids, slot_owner = jax.vmap(slot_plan)(routes.reshape(SEQS, SEQ, TOP))
    padded = jnp.concatenate([normed.reshape(SEQS, SEQ, D), jnp.zeros((SEQS, 1, D), jnp.bfloat16)], axis=1)
    sent_rows = jax.vmap(take_rows)(padded, slot_owner // TOP)
    by_expert = to_experts(sent_rows)

    def one_expert(pack):
        expert_rows, up_matrix, down_matrix = pack
        active = gelu_value(product(expert_rows, up_matrix)).astype(jnp.bfloat16)
        return product(active, down_matrix)
    outputs = to_sequences(lax.map(one_expert, (by_expert, expert_up, expert_down)))
    picked = jax.vmap(take_rows)(outputs, slot_ids).reshape(TOKENS, TOP, D)
    combined = lax.optimization_barrier(jnp.sum(picked * gate_weights[:, :, None], axis=1))
    return (hidden + combined, (normal, inv_rms, slot_ids, slot_owner, by_expert))

def expert_back(cotangent, saved, gate_weights, norm_gain, expert_up, expert_down):
    normal, inv_rms, slot_ids, slot_owner, by_expert = saved
    scaled = (gate_weights[:, :, None] * round_trip(cotangent)[:, None, :]).astype(jnp.bfloat16)
    padded = jnp.concatenate([scaled.reshape(SEQS, SEQ * TOP, D), jnp.zeros((SEQS, 1, D), jnp.bfloat16)], axis=1)
    grad_by_expert = to_experts(jax.vmap(take_rows)(padded, slot_owner))

    def one_expert(pack):
        expert_rows, grad_rows, up_matrix, down_matrix = pack
        pre_act = product(expert_rows, up_matrix)
        active = gelu_value(pre_act).astype(jnp.bfloat16)
        grad_pre = (product(grad_rows, down_matrix.T) * gelu_slope(pre_act)).astype(jnp.bfloat16)
        return (product(grad_pre, up_matrix.T), product(expert_rows.T, grad_pre), product(active.T, grad_rows))
    grad_inputs, up_grad, down_grad = lax.map(one_expert, (by_expert, grad_by_expert, expert_up, expert_down))
    picked = jax.vmap(take_rows)(to_sequences(grad_inputs), slot_ids).reshape(TOKENS, TOP, D)
    grad_normed = lax.optimization_barrier(jnp.sum(picked, axis=1))
    grad_hidden, gain_grad = norm_backward(grad_normed, normal, inv_rms, norm_gain)
    return (cotangent + grad_hidden, gain_grad, up_grad, down_grad)

def reference(layer_input, segments, routes, gate_weights, first_gain, first_query, first_key, first_value, first_output, first_bias, first_dense_gain, first_dense_up, first_dense_down, second_gain, second_query, second_key, second_value, second_output, second_bias, second_expert_gain, expert_up, expert_down, output_grad):
    hidden_one, saved_one = attention_layer(layer_input, segments, first_gain, first_query, first_key, first_value, first_output, first_bias)
    hidden_two, saved_two = dense_layer(hidden_one, first_dense_gain, first_dense_up, first_dense_down)
    hidden_three, saved_three = attention_layer(hidden_two, segments, second_gain, second_query, second_key, second_value, second_output, second_bias)
    layer_output, saved_four = expert_layer(hidden_three, routes, gate_weights, second_expert_gain, expert_up, expert_down)
    grad_three, expert_gain_grad, expert_up_grad, expert_down_grad = expert_back(output_grad, saved_four, gate_weights, second_expert_gain, expert_up, expert_down)
    grad_two, grads_two = attention_back(grad_three, saved_three, segments, second_gain, second_query, second_key, second_value, second_output, second_bias)
    grad_one, dense_gain_grad, dense_up_grad, dense_down_grad = dense_back(grad_two, saved_two, first_dense_gain, first_dense_up, first_dense_down)
    input_grad, grads_one = attention_back(grad_one, saved_one, segments, first_gain, first_query, first_key, first_value, first_output, first_bias)
    return (layer_output, input_grad, grads_one[0], grads_one[1], grads_one[2], grads_one[3], grads_one[4], grads_one[5], dense_gain_grad, dense_up_grad, dense_down_grad, grads_two[0], grads_two[1], grads_two[2], grads_two[3], grads_two[4], grads_two[5], expert_gain_grad, expert_up_grad, expert_down_grad)
```

```python
import math

import jax
import jax.numpy as jnp
import numpy as np
from jax import lax
from jax.experimental import pallas as pl
from jax.experimental.pallas import tpu as pltpu
from jax.sharding import PartitionSpec as P

DH = 64
BUCKETS = 32
EPSILON = 1e-06
NEG_FILL = -1e30
HALF_ROOT = 0.7071067811865476
BELL_SCALE = 0.3989422804014327
F32 = jnp.float32
BF16 = jnp.bfloat16


def band_onehot(length, buckets):
    exact_count = buckets // 2
    distance = np.arange(length)
    result = np.minimum(distance, exact_count)
    for bucket_level in range(1, exact_count):
        threshold = int(
            np.ceil(exact_count * (128.0 / exact_count) ** (bucket_level / exact_count))
        )
        result = result + (distance >= threshold)
    band = result[(np.arange(8)[:, None] - np.arange(length)[None, :]) % length]
    return (band.reshape(-1)[:, None] == np.arange(buckets)[None, :]).astype(np.float32)


def gelu_value(inputs):
    return 0.5 * inputs * (1.0 + lax.erf(inputs * HALF_ROOT))


def gelu_slope(inputs):
    return (
        0.5 * (1.0 + lax.erf(inputs * HALF_ROOT))
        + inputs * jnp.exp(-0.5 * inputs * inputs) * BELL_SCALE
    )


def norm_rows(token_rows, gain_full):
    values = token_rows.astype(F32)
    inv_rms = lax.rsqrt(jnp.mean(values * values, axis=-1, keepdims=True) + EPSILON)
    normal = values * inv_rms
    return ((normal * gain_full).astype(BF16), normal, inv_rms)


def norm_back(grad_normed, normal, inv_rms, gain_full):
    grad_normal = grad_normed * gain_full
    grad_part = inv_rms * (
        grad_normal - normal * jnp.mean(grad_normal * normal, axis=-1, keepdims=True)
    )
    return (grad_part, jnp.sum(grad_normed * normal, axis=0, keepdims=True))


def mm(left, right, left_dim=1, right_dim=0):
    return lax.dot_general(
        left, right, (((left_dim,), (right_dim,)), ((), ())), preferred_element_type=F32
    )


def allowed_pairs(seg_row, seg_col):
    length = seg_row.shape[1]
    rows = lax.broadcasted_iota(jnp.int32, (length, length), 0)
    cols = lax.broadcasted_iota(jnp.int32, (length, length), 1)
    return (rows >= cols) & (seg_row == seg_col)


def head_shares(query, key, band, allowed):
    length = query.shape[0]
    bias = jnp.concatenate(
        [pltpu.roll(band, 8 * step, 1) if step else band for step in range(length // 8)], axis=0
    )
    scores = mm(query, key, 1, 1) * (1.0 / math.sqrt(DH)) + bias
    scores = jnp.where(allowed, scores, NEG_FILL)
    exp_scores = jnp.exp(scores - jnp.max(scores, axis=-1, keepdims=True))
    return exp_scores / jnp.sum(exp_scores, axis=-1, keepdims=True)


def attn_forward_kernel(x_ref, g_ref, wqkv_ref, wo_ref, band_ref, segr_ref, segc_ref,
                        qkv_ref, o_ref, part_ref):
    normed, _, _ = norm_rows(x_ref[...], g_ref[...])
    qkv = mm(normed, wqkv_ref[...]).astype(BF16)
    qkv_ref[...] = qkv
    width = o_ref.shape[1]
    allowed = allowed_pairs(segr_ref[...], segc_ref[...])
    mixed = []
    for head in range(width // DH):
        lo = head * DH
        shares = head_shares(
            qkv[:, lo : lo + DH],
            qkv[:, width + lo : width + lo + DH],
            band_ref[head * 8 : head * 8 + 8, :],
            allowed,
        ).astype(BF16)
        mixed.append(mm(shares, qkv[:, 2 * width + lo : 2 * width + lo + DH]).astype(BF16))
    mixed = jnp.concatenate(mixed, axis=1)
    o_ref[...] = mixed
    part_ref[...] = mm(mixed, wo_ref[...], 1, 1).astype(BF16)


def attn_backward_kernel(b_ref, x_ref, g_ref, wqkv_ref, wo_ref, band_ref, segr_ref, segc_ref,
                         qkv_ref, o_ref, wg_ref, part_ref, gain_ref, bandg_ref):
    width = o_ref.shape[1]
    normed, normal, inv_rms = norm_rows(x_ref[...], g_ref[...])
    grad_rows = b_ref[...]
    mixed = o_ref[...]
    qkv = qkv_ref[...]
    grad_mixed = mm(grad_rows, wo_ref[...]).astype(BF16)
    allowed = allowed_pairs(segr_ref[...], segc_ref[...])
    length = qkv.shape[0]
    inv_root = 1.0 / math.sqrt(DH)
    grad_q, grad_k, grad_v = [], [], []
    for head in range(width // DH):
        lo = head * DH
        query = qkv[:, lo : lo + DH]
        key = qkv[:, width + lo : width + lo + DH]
        value = qkv[:, 2 * width + lo : 2 * width + lo + DH]
        grad_head = grad_mixed[:, lo : lo + DH]
        mixed_head = mixed[:, lo : lo + DH]
        shares = head_shares(query, key, band_ref[head * 8 : head * 8 + 8, :], allowed)
        grad_v.append(mm(shares.astype(BF16), grad_head, 0, 0).astype(BF16))
        row_dot = jnp.sum(
            grad_head.astype(F32) * mixed_head.astype(F32), axis=-1, keepdims=True
        )
        score_grad = shares * (mm(grad_head, value, 1, 1) - row_dot)
        total = score_grad[0:8, :]
        for step in range(1, length // 8):
            total = total + pltpu.roll(
                score_grad[8 * step : 8 * step + 8, :], length - 8 * step, 1
            )
        bandg_ref[head * 8 : head * 8 + 8, :] = total
        score_low = score_grad.astype(BF16)
        grad_q.append((mm(score_low, key) * inv_root).astype(BF16))
        grad_k.append((mm(score_low, query, 0, 0) * inv_root).astype(BF16))
    grad_qkv = jnp.concatenate(grad_q + grad_k + grad_v, axis=1)
    wg_ref[...] = jnp.concatenate(
        [mm(normed, grad_qkv, 0, 0).astype(BF16), mm(grad_rows, mixed, 0, 0).astype(BF16)], axis=1
    )
    grad_normed = mm(grad_qkv, wqkv_ref[...], 1, 1)
    grad_part, gain_grad = norm_back(grad_normed, normal, inv_rms, g_ref[...])
    part_ref[...] = grad_part.astype(BF16)
    gain_ref[...] = gain_grad


def dense_forward_kernel(x_ref, g_ref, w_ref, pre_ref, part_ref):
    hidden = pre_ref.shape[1]
    normed, _, _ = norm_rows(x_ref[...], g_ref[...])
    pre = mm(normed, w_ref[:, :hidden])
    pre_ref[...] = pre
    part_ref[...] = mm(gelu_value(pre).astype(BF16), w_ref[:, hidden:], 1, 1).astype(BF16)


def dense_backward_kernel(b_ref, x_ref, g_ref, w_ref, pre_ref, up_ref, down_ref, part_ref,
                          gain_ref):
    hidden = pre_ref.shape[1]
    normed, normal, inv_rms = norm_rows(x_ref[...], g_ref[...])
    grad_rows = b_ref[...]
    pre = pre_ref[...]
    active = gelu_value(pre).astype(BF16)
    down_ref[...] = mm(grad_rows, active, 0, 0).astype(BF16)
    grad_pre = (mm(grad_rows, w_ref[:, hidden:]) * gelu_slope(pre)).astype(BF16)
    up_ref[...] = mm(normed, grad_pre, 0, 0).astype(BF16)
    grad_normed = mm(grad_pre, w_ref[:, :hidden], 1, 1)
    grad_part, gain_grad = norm_back(grad_normed, normal, inv_rms, g_ref[...])
    part_ref[...] = grad_part.astype(BF16)
    gain_ref[...] = gain_grad


def call(kernel, outs, *args):
    return pl.pallas_call(
        kernel,
        out_shape=[jax.ShapeDtypeStruct(shape, dtype) for shape, dtype in outs],
        compiler_params=pltpu.CompilerParams(vmem_limit_bytes=40 * 1024 * 1024),
    )(*args)


def gather_rows(hidden):
    return lax.all_gather(hidden.astype(BF16), "tensor", axis=0, tiled=True)


def swap_sum(parts, axis_name, count):
    blocks = parts.astype(BF16).reshape(count, parts.shape[0] // count, parts.shape[1])
    arrived = lax.all_to_all(blocks, axis_name, split_axis=0, concat_axis=0, tiled=True)
    return jnp.sum(arrived.astype(F32), axis=0)


def swap_blocks(blocks):
    return lax.all_to_all(blocks, "dp", split_axis=0, concat_axis=0, tiled=True)


def slot_plan(routes, expert_count, capacity):
    length, top_count = routes.shape
    flat_routes = routes.reshape(-1)
    onehot = (flat_routes[:, None] == jnp.arange(expert_count, dtype=jnp.int32)[None, :]).astype(
        jnp.int32
    )
    before = jnp.cumsum(onehot, axis=0) - onehot
    slot_ids = flat_routes * capacity + jnp.sum(onehot * before, axis=1)
    return slot_ids.reshape(length, top_count)


def on_device(
    layer_input, segments, routes, gate_weights,
    first_gain, first_query, first_key, first_value, first_output, first_bias,
    first_dense_gain, first_dense_up, first_dense_down,
    second_gain, second_query, second_key, second_value, second_output, second_bias,
    second_expert_gain, expert_up, expert_down, output_grad,
):
    dp_count, tensor_count = lax.axis_size("dp"), lax.axis_size("tensor")
    dp_index, tensor_index = lax.axis_index("dp"), lax.axis_index("tensor")
    length = segments.shape[1]
    features = layer_input.shape[1]
    width = first_query.shape[1]
    heads = first_bias.shape[1]
    hidden = first_dense_up.shape[1]
    piece = first_gain.shape[0]
    bias_rows = first_bias.shape[0]
    table = jnp.asarray(band_onehot(length, BUCKETS))

    small = jnp.concatenate(
        [first_gain, first_dense_gain, second_gain, second_expert_gain,
         first_bias.reshape(-1), second_bias.reshape(-1)]
    )
    pad = (-small.shape[0]) % 128
    small = jnp.pad(small, (0, pad))
    smalls = lax.all_gather(small[None], ("dp", "tensor"), axis=0, tiled=True)
    gains = [
        smalls[:, k * piece : (k + 1) * piece].astype(F32).reshape(1, features) for k in range(4)
    ]
    biases = []
    for k in range(2):
        start = 4 * piece + k * bias_rows * heads
        block = smalls[:, start : start + bias_rows * heads].reshape(
            dp_count, tensor_count, bias_rows, heads
        )
        biases.append(
            lax.dynamic_index_in_dim(block, tensor_index, 1, keepdims=False).reshape(
                dp_count * bias_rows, heads
            )
        )
    bands = [
        jnp.dot(table, bias.astype(F32), precision=lax.Precision.HIGHEST).T.reshape(
            heads * 8, length
        )
        for bias in biases
    ]

    def fetch(*parts):
        return lax.all_gather(jnp.concatenate(parts, axis=1), "dp", axis=0, tiled=True)

    weights_one = fetch(first_query, first_key, first_value, first_output.T)
    weights_dense = fetch(first_dense_up, first_dense_down.T)
    weights_two = fetch(second_query, second_key, second_value, second_output.T)
    seg_row = segments
    seg_col = segments.reshape(length, 1)

    def attn_forward(x_rows, gain, weights, band):
        wqkv, wo = weights[:, : 3 * width], weights[:, 3 * width :]
        qkv, mixed, part = call(
            attn_forward_kernel,
            [((length, 3 * width), BF16), ((length, width), BF16), ((length, features), BF16)],
            x_rows, gain, wqkv, wo, band, seg_row, seg_col,
        )
        return part, (x_rows, gain, wqkv, wo, band, qkv, mixed)

    def attn_backward(grad_rows, saved):
        x_rows, gain, wqkv, wo, band, qkv, mixed = saved
        return call(
            attn_backward_kernel,
            [((features, 4 * width), BF16), ((length, features), BF16), ((1, features), F32),
             ((heads * 8, length), F32)],
            grad_rows, x_rows, gain, wqkv, wo, band, seg_row, seg_col, qkv, mixed,
        )

    def collect(part):
        return swap_sum(part, "tensor", tensor_count)

    top_count = routes.shape[1]
    local_experts = expert_up.shape[0]
    expert_count = local_experts * dp_count
    capacity = max(2, 3 * length * top_count // (2 * expert_count))
    slots = expert_count * capacity
    slot_ids = slot_plan(routes, expert_count, capacity)
    slot_flat = slot_ids.T.reshape(1, top_count * length)
    place = (jnp.arange(slots, dtype=jnp.int32)[:, None] == slot_flat).astype(BF16)
    place_rows = place.reshape(slots, top_count, length).sum(axis=1)
    sent_shape = (dp_count, local_experts, capacity, features)

    out_grad_rows = gather_rows(output_grad)
    scaled = (gate_weights.T[:, :, None] * out_grad_rows.astype(F32)[None]).astype(BF16)
    sent_grad = mm(place, scaled.reshape(top_count * length, features)).astype(BF16)
    arrived_grad = swap_blocks(sent_grad.reshape(sent_shape))

    part, saved_one = attn_forward(gather_rows(layer_input), gains[0], weights_one, bands[0])
    hidden_one = layer_input + collect(part)
    rows_one = gather_rows(hidden_one)
    pre_act, part = call(
        dense_forward_kernel,
        [((length, hidden), F32), ((length, features), BF16)],
        rows_one, gains[1], weights_dense,
    )
    hidden_two = hidden_one + collect(part)
    part, saved_three = attn_forward(gather_rows(hidden_two), gains[2], weights_two, bands[1])
    hidden_three = hidden_two + collect(part)
    rows_three = gather_rows(hidden_three)
    normed, normal, inv_rms = norm_rows(rows_three, gains[3])
    arrived = swap_blocks(mm(place_rows, normed).astype(BF16).reshape(sent_shape))
    pre_expert = jnp.einsum("secd,edf->secf", arrived, expert_up, preferred_element_type=F32)

    grad_active = jnp.einsum(
        "secd,efd->secf", arrived_grad, expert_down, preferred_element_type=F32
    )
    grad_pre = (grad_active * gelu_slope(pre_expert)).astype(BF16)
    grad_sent = jnp.einsum(
        "secf,edf->secd", grad_pre, expert_up, preferred_element_type=F32
    ).astype(BF16)
    grad_back = swap_blocks(grad_sent).reshape(slots, features)
    grad_normed = mm(place_rows, grad_back, 0, 0)
    grad_part, expert_gain_grad = norm_back(grad_normed, normal, inv_rms, gains[3])
    grad_three = output_grad + collect(grad_part)

    active = gelu_value(pre_expert).astype(BF16)
    expert_rows = jnp.einsum(
        "secf,efd->secd", active, expert_down, preferred_element_type=F32
    ).astype(BF16)
    returned = swap_blocks(expert_rows).reshape(slots, features)
    picked = mm(place, returned, 0, 0).reshape(top_count, length, features)
    combined = jnp.sum(picked * gate_weights.T[:, :, None], axis=0)
    layer_output = hidden_three + collect(combined)
    expert_down_grad = jnp.einsum("secf,secd->efd", active, arrived_grad, preferred_element_type=F32)
    expert_up_grad = jnp.einsum("secd,secf->edf", arrived, grad_pre, preferred_element_type=F32)

    wg_two, part, gain_two, band_grad_two = attn_backward(gather_rows(grad_three), saved_three)
    summed_two = swap_sum(wg_two, "dp", dp_count)
    grad_two = grad_three + collect(part)
    up_wg, down_wg, part, gain_dense = call(
        dense_backward_kernel,
        [((features, hidden), BF16), ((features, hidden), BF16), ((length, features), BF16),
         ((1, features), F32)],
        gather_rows(grad_two), rows_one, gains[1], weights_dense, pre_act,
    )
    dense_up_grad = swap_sum(up_wg, "dp", dp_count)
    dense_down_grad = swap_sum(down_wg, "dp", dp_count).T
    grad_one = grad_two + collect(part)
    wg_one, part, gain_one, band_grad_one = attn_backward(gather_rows(grad_one), saved_one)
    summed_one = swap_sum(wg_one, "dp", dp_count)
    grad_zero = grad_one + collect(part)

    mine = (jnp.arange(tensor_count) == tensor_index).astype(F32)

    def spread_bias(band_grad):
        grad = jnp.dot(
            table.T, band_grad.reshape(heads, 8 * length).T, precision=lax.Precision.HIGHEST
        )
        return (grad[:, None, :] * mine[None, :, None]).reshape(-1)

    totals = lax.psum(
        jnp.concatenate(
            [gain_one[0], gain_dense[0], gain_two[0], expert_gain_grad[0],
             spread_bias(band_grad_one), spread_bias(band_grad_two)]
        ),
        ("dp", "tensor"),
    )
    own = (dp_index * tensor_count + tensor_index) * piece
    gain_grads = [
        lax.dynamic_slice_in_dim(totals, k * features + own, piece) for k in range(4)
    ]
    bias_grads = [
        lax.dynamic_slice(
            grad, (dp_index * bias_rows, tensor_index * heads), (bias_rows, heads)
        )
        for grad in totals[4 * features :].reshape(2, BUCKETS, tensor_count * heads)
    ]

    def split_four(summed):
        return (
            summed[:, :width],
            summed[:, width : 2 * width],
            summed[:, 2 * width : 3 * width],
            summed[:, 3 * width :].T,
        )

    return (
        layer_output,
        grad_zero,
        gain_grads[0],
        *split_four(summed_one),
        bias_grads[0],
        gain_grads[1],
        dense_up_grad,
        dense_down_grad,
        gain_grads[2],
        *split_four(summed_two),
        bias_grads[1],
        gain_grads[3],
        expert_up_grad,
        expert_down_grad,
    )


def solution(mesh):
    attn = (P("dp", "tensor"), P("dp", "tensor"), P("dp", "tensor"), P("tensor", "dp"),
            P("dp", "tensor"))
    both = P(("dp", "tensor"))
    rows = P(("dp", "tensor"), None)
    return jax.shard_map(
        on_device,
        mesh=mesh,
        in_specs=(
            rows, P("dp", None), P("dp", None), P("dp", None),
            both, *attn,
            both, P("dp", "tensor"), P("tensor", "dp"),
            both, *attn,
            both, P("dp", None, "tensor"), P("dp", "tensor", None), rows,
        ),
        out_specs=(
            rows, rows,
            both, *attn,
            both, P("dp", "tensor"), P("tensor", "dp"),
            both, *attn,
            both, P("dp", None, "tensor"), P("dp", "tensor", None),
        ),
        check_vma=False,
    )
```

```python
import functools
import math

import jax
import jax.numpy as jnp
import numpy as np
from jax import lax
from jax.experimental import pallas as pl
from jax.experimental.pallas import tpu as pltpu
from jax.sharding import PartitionSpec as P

DH = 64
BUCKETS = 32
EPSILON = 1e-06
NEG_FILL = -1e30
HALF_ROOT = 0.7071067811865476
BELL_SCALE = 0.3989422804014327
F32 = jnp.float32
BF16 = jnp.bfloat16


def band_onehot(length, buckets):
    exact_count = buckets // 2
    distance = np.arange(length)
    result = np.minimum(distance, exact_count)
    for bucket_level in range(1, exact_count):
        threshold = int(
            np.ceil(exact_count * (128.0 / exact_count) ** (bucket_level / exact_count))
        )
        result = result + (distance >= threshold)
    band = result[(np.arange(8)[:, None] - np.arange(length)[None, :]) % length]
    return (band.reshape(-1)[:, None] == np.arange(buckets)[None, :]).astype(np.float32)


def gelu_value(inputs):
    return 0.5 * inputs * (1.0 + lax.erf(inputs * HALF_ROOT))


def gelu_slope(inputs):
    return (
        0.5 * (1.0 + lax.erf(inputs * HALF_ROOT))
        + inputs * jnp.exp(-0.5 * inputs * inputs) * BELL_SCALE
    )


def norm_rows(token_rows, gain_full):
    values = token_rows.astype(F32)
    inv_rms = lax.rsqrt(jnp.mean(values * values, axis=-1, keepdims=True) + EPSILON)
    normal = values * inv_rms
    return ((normal * gain_full).astype(BF16), normal, inv_rms)


def norm_back(grad_normed, normal, inv_rms, gain_full):
    grad_normal = grad_normed * gain_full
    grad_part = inv_rms * (
        grad_normal - normal * jnp.mean(grad_normal * normal, axis=-1, keepdims=True)
    )
    return (grad_part, jnp.sum(grad_normed * normal, axis=0, keepdims=True))


def mm(left, right, left_dim=1, right_dim=0):
    return lax.dot_general(
        left, right, (((left_dim,), (right_dim,)), ((), ())), preferred_element_type=F32
    )


def allowed_pairs(seg_row, seg_col):
    length = seg_row.shape[1]
    rows = lax.broadcasted_iota(jnp.int32, (length, length), 0)
    cols = lax.broadcasted_iota(jnp.int32, (length, length), 1)
    return (rows >= cols) & (seg_row == seg_col)


def head_shares(query, key, band, allowed):
    length = query.shape[0]
    bias = jnp.concatenate(
        [pltpu.roll(band, 8 * step, 1) if step else band for step in range(length // 8)], axis=0
    )
    scores = mm(query, key, 1, 1) * (1.0 / math.sqrt(DH)) + bias
    scores = jnp.where(allowed, scores, NEG_FILL)
    exp_scores = jnp.exp(scores - jnp.max(scores, axis=-1, keepdims=True))
    return exp_scores / jnp.sum(exp_scores, axis=-1, keepdims=True)


def attn_forward_kernel(x_ref, g_ref, w_ref, band_ref, segr_ref, segc_ref,
                        qkv_ref, o_ref, part_ref):
    normed, _, _ = norm_rows(x_ref[...], g_ref[...])
    width = o_ref.shape[1]
    weights = w_ref[...]
    qkv = mm(normed, weights[:, : 3 * width]).astype(BF16)
    qkv_ref[...] = qkv
    allowed = allowed_pairs(segr_ref[...], segc_ref[...])
    mixed = []
    for head in range(width // DH):
        lo = head * DH
        shares = head_shares(
            qkv[:, lo : lo + DH],
            qkv[:, width + lo : width + lo + DH],
            band_ref[head * 8 : head * 8 + 8, :],
            allowed,
        ).astype(BF16)
        mixed.append(mm(shares, qkv[:, 2 * width + lo : 2 * width + lo + DH]).astype(BF16))
    mixed = jnp.concatenate(mixed, axis=1)
    o_ref[...] = mixed
    part_ref[...] = mm(mixed, weights[:, 3 * width :], 1, 1).astype(BF16)


def attn_backward_kernel(b_ref, x_ref, g_ref, w_ref, band_ref, segr_ref, segc_ref,
                         qkv_ref, o_ref, wg_ref, part_ref, gain_ref, bandg_ref):
    width = o_ref.shape[1]
    normed, normal, inv_rms = norm_rows(x_ref[...], g_ref[...])
    grad_rows = b_ref[...]
    mixed = o_ref[...]
    qkv = qkv_ref[...]
    weights = w_ref[...]
    grad_mixed = mm(grad_rows, weights[:, 3 * width :]).astype(BF16)
    allowed = allowed_pairs(segr_ref[...], segc_ref[...])
    length = qkv.shape[0]
    inv_root = 1.0 / math.sqrt(DH)
    grad_q, grad_k, grad_v = [], [], []
    for head in range(width // DH):
        lo = head * DH
        query = qkv[:, lo : lo + DH]
        key = qkv[:, width + lo : width + lo + DH]
        value = qkv[:, 2 * width + lo : 2 * width + lo + DH]
        grad_head = grad_mixed[:, lo : lo + DH]
        mixed_head = mixed[:, lo : lo + DH]
        shares = head_shares(query, key, band_ref[head * 8 : head * 8 + 8, :], allowed)
        grad_v.append(mm(shares.astype(BF16), grad_head, 0, 0).astype(BF16))
        row_dot = jnp.sum(
            grad_head.astype(F32) * mixed_head.astype(F32), axis=-1, keepdims=True
        )
        score_grad = shares * (mm(grad_head, value, 1, 1) - row_dot)
        total = score_grad[0:8, :]
        for step in range(1, length // 8):
            total = total + pltpu.roll(
                score_grad[8 * step : 8 * step + 8, :], length - 8 * step, 1
            )
        bandg_ref[head * 8 : head * 8 + 8, :] = total
        score_low = score_grad.astype(BF16)
        grad_q.append((mm(score_low, key) * inv_root).astype(BF16))
        grad_k.append((mm(score_low, query, 0, 0) * inv_root).astype(BF16))
    grad_qkv = jnp.concatenate(grad_q + grad_k + grad_v, axis=1)
    wg_ref[...] = jnp.concatenate(
        [mm(normed, grad_qkv, 0, 0).astype(BF16), mm(grad_rows, mixed, 0, 0).astype(BF16)], axis=1
    )
    grad_normed = mm(grad_qkv, weights[:, : 3 * width], 1, 1)
    grad_part, gain_grad = norm_back(grad_normed, normal, inv_rms, g_ref[...])
    part_ref[...] = grad_part.astype(BF16)
    gain_ref[...] = jnp.broadcast_to(gain_grad, gain_ref.shape)


def dense_forward_kernel(x_ref, g_ref, w_ref, pre_ref, part_ref):
    hidden = pre_ref.shape[1]
    normed, _, _ = norm_rows(x_ref[...], g_ref[...])
    pre = mm(normed, w_ref[:, :hidden])
    pre_ref[...] = pre
    part_ref[...] = mm(gelu_value(pre).astype(BF16), w_ref[:, hidden:], 1, 1).astype(BF16)


def dense_backward_kernel(b_ref, x_ref, g_ref, w_ref, pre_ref, up_ref, down_ref, part_ref,
                          gain_ref):
    hidden = pre_ref.shape[1]
    normed, normal, inv_rms = norm_rows(x_ref[...], g_ref[...])
    grad_rows = b_ref[...]
    pre = pre_ref[...]
    active = gelu_value(pre).astype(BF16)
    down_ref[...] = mm(grad_rows, active, 0, 0).astype(BF16)
    grad_pre = (mm(grad_rows, w_ref[:, hidden:]) * gelu_slope(pre)).astype(BF16)
    up_ref[...] = mm(normed, grad_pre, 0, 0).astype(BF16)
    grad_normed = mm(grad_pre, w_ref[:, :hidden], 1, 1)
    grad_part, gain_grad = norm_back(grad_normed, normal, inv_rms, g_ref[...])
    part_ref[...] = grad_part.astype(BF16)
    gain_ref[...] = jnp.broadcast_to(gain_grad, gain_ref.shape)


def call(kernel, outs, *args):
    return pl.pallas_call(
        kernel,
        out_shape=[jax.ShapeDtypeStruct(shape, dtype) for shape, dtype in outs],
        compiler_params=pltpu.CompilerParams(vmem_limit_bytes=40 * 1024 * 1024),
    )(*args)


def greet_peers(count):
    me = lax.axis_index("tensor")
    barrier = pltpu.get_barrier_semaphore()
    for offset in range(1, count):
        pl.semaphore_signal(
            barrier, inc=1, device_id={"tensor": lax.rem(me + offset, count)},
            device_id_type=pl.DeviceIdType.MESH,
        )
    pl.semaphore_wait(barrier, count - 1)
    return me


def remote(source, target, send_sem, recv_sem, peer):
    return pltpu.make_async_remote_copy(
        src_ref=source, dst_ref=target, send_sem=send_sem, recv_sem=recv_sem,
        device_id={"tensor": peer}, device_id_type=pl.DeviceIdType.MESH,
    )


def gather_kernel(count, x_ref, g_ref, s_ref, xo_ref, go_ref, so_ref, send_sem, recv_sem):
    me = greet_peers(count)
    block = x_ref.shape[0]
    own = pl.ds(pl.multiple_of(me * block, block), block)
    xo_ref[own, :] = x_ref[...].astype(BF16)
    go_ref[own, :] = g_ref[...].astype(BF16)
    so_ref[pl.ds(me, 1)] = s_ref[...][None]
    copies = []
    for kind, (source, target) in enumerate([
        (s_ref, so_ref.at[me]),
        (xo_ref.at[own, :], xo_ref.at[own, :]),
        (go_ref.at[own, :], go_ref.at[own, :]),
    ]):
        for offset in range(1, count):
            copy = remote(source, target, send_sem.at[kind, offset], recv_sem.at[kind, offset],
                          lax.rem(me + offset, count))
            copy.start()
            copies.append(copy)
    for copy in copies:
        copy.wait()


def boundary_kernel(count, with_gain, spread, *refs):
    refs = list(refs)
    part_ref, resid_ref = refs[:2]
    refs = refs[2:]
    gain_ref = refs.pop(0) if with_gain else None
    out_ref = refs.pop(0)
    rows_ref = refs.pop(0) if spread else None
    gain_out = refs.pop(0) if with_gain else None
    land = refs.pop(0)
    gain_land = refs.pop(0) if with_gain else None
    send_sem, recv_sem = refs
    me = greet_peers(count)
    block = out_ref.shape[0]
    own = pl.ds(pl.multiple_of(me * block, block), block)
    copies, gain_copies = [], []
    for offset in range(1, count):
        peer = lax.rem(me + offset, count)
        copy = remote(
            part_ref.at[pl.ds(pl.multiple_of(peer * block, block), block), :],
            land.at[offset - 1], send_sem.at[0, offset], recv_sem.at[0, offset], peer,
        )
        copy.start()
        copies.append(copy)
    if with_gain:
        for offset in range(1, count):
            copy = remote(gain_ref, gain_land.at[offset - 1], send_sem.at[1, offset],
                          recv_sem.at[1, offset], lax.rem(me + offset, count))
            copy.start()
            gain_copies.append(copy)
    total = part_ref[own, :].astype(F32)
    for offset, copy in enumerate(copies):
        copy.wait_recv()
        total = total + land[offset].astype(F32)
    total = resid_ref[...] + total
    out_ref[...] = total
    if spread:
        rows_ref[own, :] = total.astype(BF16)
        for offset in range(1, count):
            copy = remote(rows_ref.at[own, :], rows_ref.at[own, :], send_sem.at[2, offset],
                          recv_sem.at[2, offset], lax.rem(me + offset, count))
            copy.start()
            gain_copies.append(copy)
    for copy in copies:
        copy.wait_send()
    for copy in gain_copies:
        copy.wait()
    if with_gain:
        gain_total = gain_ref[...]
        for offset in range(count - 1):
            gain_total = gain_total + gain_land[offset]
        gain_out[...] = gain_total


def comm_call(kernel, number, outs, scratch, *args):
    vmem = pl.BlockSpec(memory_space=pltpu.VMEM)
    return pl.pallas_call(
        kernel,
        out_shape=[jax.ShapeDtypeStruct(shape, dtype) for shape, dtype in outs],
        in_specs=[vmem] * len(args),
        out_specs=[vmem] * len(outs),
        scratch_shapes=scratch,
        compiler_params=pltpu.CompilerParams(collective_id=number, has_side_effects=True),
    )(*args)


def boundary(number, part, resid, gain=None, spread=True):
    count = lax.axis_size("tensor")
    block, features = resid.shape
    outs = [((block, features), F32)]
    if spread:
        outs.append((part.shape, BF16))
    scratch = [pltpu.VMEM((count - 1, block, features), BF16)]
    args = [part, resid]
    if gain is not None:
        outs.append((gain.shape, F32))
        scratch.append(pltpu.VMEM((count - 1, *gain.shape), F32))
        args.append(gain)
    scratch += [pltpu.SemaphoreType.DMA((3, count)), pltpu.SemaphoreType.DMA((3, count))]
    return comm_call(
        functools.partial(boundary_kernel, count, gain is not None, spread),
        number, outs, scratch, *args,
    )


def swap_sum(parts, axis_name, count):
    blocks = parts.astype(BF16).reshape(count, parts.shape[0] // count, parts.shape[1])
    arrived = lax.all_to_all(blocks, axis_name, split_axis=0, concat_axis=0, tiled=True)
    return jnp.sum(arrived.astype(F32), axis=0)


def swap_blocks(blocks):
    return lax.all_to_all(blocks, "dp", split_axis=0, concat_axis=0, tiled=True)


def slot_plan(routes, expert_count, capacity):
    length, top_count = routes.shape
    flat_routes = routes.reshape(-1)
    onehot = (flat_routes[:, None] == jnp.arange(expert_count, dtype=jnp.int32)[None, :]).astype(
        BF16
    )
    pairs = jnp.arange(length * top_count, dtype=jnp.int32)
    before = mm((pairs[:, None] > pairs[None, :]).astype(BF16), onehot)
    earlier = jnp.sum(onehot.astype(F32) * before, axis=1).astype(jnp.int32)
    slot_ids = flat_routes * capacity + earlier
    return slot_ids.reshape(length, top_count)


def on_device(
    layer_input, segments, routes, gate_weights,
    first_gain, first_query, first_key, first_value, first_output, first_bias,
    first_dense_gain, first_dense_up, first_dense_down,
    second_gain, second_query, second_key, second_value, second_output, second_bias,
    second_expert_gain, expert_up, expert_down, output_grad,
):
    dp_count, tensor_count = lax.axis_size("dp"), lax.axis_size("tensor")
    tensor_index = lax.axis_index("tensor")
    length = segments.shape[1]
    features = layer_input.shape[1]
    width = first_query.shape[1]
    heads = first_bias.shape[1]
    hidden = first_dense_up.shape[1]
    piece = first_gain.shape[0]
    bias_rows = first_bias.shape[0]
    table = jnp.asarray(band_onehot(length, BUCKETS))

    small = jnp.concatenate(
        [first_gain, first_dense_gain, second_gain, second_expert_gain,
         first_bias.reshape(-1), second_bias.reshape(-1)]
    )
    pad = (-small.shape[0]) % 128
    small = jnp.pad(small, (0, pad))
    rows_zero, out_grad_rows, smalls = comm_call(
        functools.partial(gather_kernel, tensor_count), 1,
        [((length, features), BF16), ((length, features), BF16),
         ((tensor_count, 8, small.shape[0]), F32)],
        [pltpu.SemaphoreType.DMA((3, tensor_count)), pltpu.SemaphoreType.DMA((3, tensor_count))],
        layer_input, output_grad,
        jnp.broadcast_to(small.astype(F32)[None], (8, small.shape[0])),
    )
    smalls = lax.all_gather(smalls[:, 0, :].astype(BF16), "dp", axis=0, tiled=True)
    gains = [
        smalls[:, k * piece : (k + 1) * piece].astype(F32).reshape(1, features) for k in range(4)
    ]
    biases = []
    for k in range(2):
        start = 4 * piece + k * bias_rows * heads
        block = smalls[:, start : start + bias_rows * heads].reshape(
            dp_count, tensor_count, bias_rows, heads
        )
        biases.append(
            lax.dynamic_index_in_dim(block, tensor_index, 1, keepdims=False).reshape(
                dp_count * bias_rows, heads
            )
        )
    bands = [
        jnp.dot(table, bias.astype(F32), precision=lax.Precision.HIGHEST).T.reshape(
            heads * 8, length
        )
        for bias in biases
    ]

    def fetch(*parts):
        return lax.all_gather(jnp.concatenate(parts, axis=1), "dp", axis=0, tiled=True)

    weights_one = fetch(first_query, first_key, first_value, first_output.T)
    weights_dense = fetch(first_dense_up, first_dense_down.T)
    weights_two = fetch(second_query, second_key, second_value, second_output.T)
    seg_row = segments
    seg_col = segments.reshape(length, 1)

    def attn_forward(x_rows, gain, weights, band):
        qkv, mixed, part = call(
            attn_forward_kernel,
            [((length, 3 * width), BF16), ((length, width), BF16), ((length, features), BF16)],
            x_rows, gain, weights, band, seg_row, seg_col,
        )
        return part, (x_rows, gain, weights, band, qkv, mixed)

    def attn_backward(grad_rows, saved):
        x_rows, gain, weights, band, qkv, mixed = saved
        return call(
            attn_backward_kernel,
            [((features, 4 * width), BF16), ((length, features), BF16), ((8, features), F32),
             ((heads * 8, length), F32)],
            grad_rows, x_rows, gain, weights, band, seg_row, seg_col, qkv, mixed,
        )

    top_count = routes.shape[1]
    local_experts = expert_up.shape[0]
    expert_count = local_experts * dp_count
    capacity = max(2, 3 * length * top_count // (2 * expert_count))
    slots = expert_count * capacity
    slot_ids = slot_plan(routes, expert_count, capacity)
    slot_flat = slot_ids.T.reshape(1, top_count * length)
    place = (jnp.arange(slots, dtype=jnp.int32)[:, None] == slot_flat).astype(BF16)
    place_rows = place.reshape(slots, top_count, length).sum(axis=1)
    sent_shape = (dp_count, local_experts, capacity, features)

    scaled = (gate_weights.T[:, :, None] * out_grad_rows.astype(F32)[None]).astype(BF16)
    sent_grad = mm(place, scaled.reshape(top_count * length, features)).astype(BF16)
    arrived_grad = swap_blocks(sent_grad.reshape(sent_shape))

    part, saved_one = attn_forward(rows_zero, gains[0], weights_one, bands[0])
    hidden_one, rows_one = boundary(2, part, layer_input)
    pre_act, part = call(
        dense_forward_kernel,
        [((length, hidden), F32), ((length, features), BF16)],
        rows_one, gains[1], weights_dense,
    )
    part, arrived_grad = lax.optimization_barrier((part, arrived_grad))
    hidden_two, rows_two = boundary(2, part, hidden_one)
    part, saved_three = attn_forward(rows_two, gains[2], weights_two, bands[1])
    hidden_three, rows_three = boundary(2, part, hidden_two)
    normed, normal, inv_rms = norm_rows(rows_three, gains[3])
    arrived = swap_blocks(mm(place_rows, normed).astype(BF16).reshape(sent_shape))
    pre_expert = jnp.einsum("secd,edf->secf", arrived, expert_up, preferred_element_type=F32)

    grad_active = jnp.einsum(
        "secd,efd->secf", arrived_grad, expert_down, preferred_element_type=F32
    )
    grad_pre = (grad_active * gelu_slope(pre_expert)).astype(BF16)
    grad_sent = jnp.einsum(
        "secf,edf->secd", grad_pre, expert_up, preferred_element_type=F32
    ).astype(BF16)
    grad_back = swap_blocks(grad_sent).reshape(slots, features)
    grad_normed = mm(place_rows, grad_back, 0, 0)
    grad_part, expert_gain_grad = norm_back(grad_normed, normal, inv_rms, gains[3])
    grad_three, grad_rows_three, gain_expert = boundary(
        3, grad_part.astype(BF16), output_grad,
        jnp.broadcast_to(expert_gain_grad, (8, features)),
    )

    active = gelu_value(pre_expert).astype(BF16)
    expert_rows = jnp.einsum(
        "secf,efd->secd", active, expert_down, preferred_element_type=F32
    ).astype(BF16)
    returned = swap_blocks(expert_rows).reshape(slots, features)
    picked = mm(place, returned, 0, 0).reshape(top_count, length, features)
    combined = jnp.sum(picked * gate_weights.T[:, :, None], axis=0)
    (layer_output,) = boundary(4, combined.astype(BF16), hidden_three, spread=False)
    expert_down_grad = jnp.einsum("secf,secd->efd", active, arrived_grad, preferred_element_type=F32)
    expert_up_grad = jnp.einsum("secd,secf->edf", arrived, grad_pre, preferred_element_type=F32)

    wg_two, part, gain_two, band_grad_two = attn_backward(grad_rows_three, saved_three)
    summed_two = swap_sum(wg_two, "dp", dp_count)
    grad_two, grad_rows_two, gain_two = boundary(3, part, grad_three, gain_two)
    up_wg, down_wg, part, gain_dense = call(
        dense_backward_kernel,
        [((features, hidden), BF16), ((features, hidden), BF16), ((length, features), BF16),
         ((8, features), F32)],
        grad_rows_two, rows_one, gains[1], weights_dense, pre_act,
    )
    dense_up_grad = swap_sum(up_wg, "dp", dp_count)
    dense_down_grad = swap_sum(down_wg, "dp", dp_count).T
    grad_one, grad_rows_one, gain_dense = boundary(3, part, grad_two, gain_dense)
    wg_one, part, gain_one, band_grad_one = attn_backward(grad_rows_one, saved_one)
    summed_one = swap_sum(wg_one, "dp", dp_count)
    grad_zero, gain_one = boundary(5, part, grad_one, gain_one, spread=False)

    def bias_block(band_grad):
        grad = jnp.dot(
            table.T, band_grad.reshape(heads, 8 * length).T, precision=lax.Precision.HIGHEST
        )
        return grad.reshape(dp_count, bias_rows * heads)

    def gain_block(gain_sum):
        block = gain_sum[0].reshape(dp_count, tensor_count, piece)
        return lax.dynamic_index_in_dim(block, tensor_index, 1, keepdims=False)

    sent_small = jnp.concatenate(
        [gain_block(gain) for gain in (gain_one, gain_dense, gain_two, gain_expert)]
        + [bias_block(band_grad_one), bias_block(band_grad_two)],
        axis=1,
    )
    sent_small = jnp.pad(sent_small, ((0, 0), (0, pad)))
    totals = jnp.sum(
        lax.all_to_all(sent_small, "dp", split_axis=0, concat_axis=0, tiled=True), axis=0
    )
    gain_grads = [totals[k * piece : (k + 1) * piece] for k in range(4)]
    bias_grads = [
        totals[4 * piece + k * bias_rows * heads :][: bias_rows * heads].reshape(bias_rows, heads)
        for k in range(2)
    ]

    def split_four(summed):
        return (
            summed[:, :width],
            summed[:, width : 2 * width],
            summed[:, 2 * width : 3 * width],
            summed[:, 3 * width :].T,
        )

    return (
        layer_output,
        grad_zero,
        gain_grads[0],
        *split_four(summed_one),
        bias_grads[0],
        gain_grads[1],
        dense_up_grad,
        dense_down_grad,
        gain_grads[2],
        *split_four(summed_two),
        bias_grads[1],
        gain_grads[3],
        expert_up_grad,
        expert_down_grad,
    )


def solution(mesh):
    attn = (P("dp", "tensor"), P("dp", "tensor"), P("dp", "tensor"), P("tensor", "dp"),
            P("dp", "tensor"))
    both = P(("dp", "tensor"))
    rows = P(("dp", "tensor"), None)
    return jax.shard_map(
        on_device,
        mesh=mesh,
        in_specs=(
            rows, P("dp", None), P("dp", None), P("dp", None),
            both, *attn,
            both, P("dp", "tensor"), P("tensor", "dp"),
            both, *attn,
            both, P("dp", None, "tensor"), P("dp", "tensor", None), rows,
        ),
        out_specs=(
            rows, rows,
            both, *attn,
            both, P("dp", "tensor"), P("tensor", "dp"),
            both, *attn,
            both, P("dp", None, "tensor"), P("dp", "tensor", None),
        ),
        check_vma=False,
    )
```
